128 devices in a mesh: seq: 32 (over y, z, core), exp: 4 (over x).
Axes of the slice: x: 4, y: 4, z: 4, core: 2. Of those that a mesh axis runs over, the one named last changes fastest.
Arguments:
- query_proj: bfloat16 [8192, 2048], P('seq', 'exp'), may hold values from -6 to 6
- key_proj: bfloat16 [8192, 2048], P('seq', 'exp'), may hold values from -6 to 6
- value_proj: bfloat16 [8192, 4096], P('seq', 'exp'), may hold values from -6 to 6
- result_valve_maps: bfloat16 [8192, 4096], P('seq', 'exp'), may hold values from -6 to 6
- beta_logit: float32 [8192, 32], P('seq', 'exp'), may hold values from -12 to 3
- decay_logit: float32 [8192, 32], P('seq', 'exp'), may hold values from -8 to 16414
- decay_rate: float32 [32], P('exp'), may hold values from 0 to 0.06
- conv_query: float32 [4, 2048], P(None, 'exp'), may hold values from -3 to 3
- conv_key: float32 [4, 2048], P(None, 'exp'), may hold values from -3 to 3
- conv_value: float32 [4, 4096], P(None, 'exp'), may hold values from -3 to 3
- norm_gain: float32 [128], replicated, may hold values from 0.1 to 1.9
- output_weight: bfloat16 [4096, 2048], P('exp'), may hold values from -0.09375 to 0.09375
- residual: bfloat16 [8192, 2048], P(('seq', 'exp')), may hold values from -6 to 6
- post_gain: float32 [2048], replicated, may hold values from 0.1 to 1.9
- route_experts: int32 [8192, 10], P(('seq', 'exp')), may hold values from 0 to 255, all different within a row; in each aligned block of 64 rows (0 to 63, 64 to 127, ...) at most 6 rows name the same one
- route_weights: float32 [8192, 10], P(('seq', 'exp')), may hold values from 0.05 to 1
- expert_gate: bfloat16 [256, 2048, 512], P(('seq', 'exp')), may hold values from -0.125 to 0.125
- expert_up: bfloat16 [256, 2048, 512], P(('seq', 'exp')), may hold values from -0.125 to 0.125
- expert_down: bfloat16 [256, 512, 2048], P(('seq', 'exp')), may hold values from -0.25 to 0.25
Outputs:
- mixer_out: bfloat16 [8192, 2048], P(('seq', 'exp'))
- expert_mixture: bfloat16 [8192, 2048], P(('seq', 'exp'))
The draws below stay inside these ranges and needn't reach their ends.
Inputs may be any that keep to these rules, and one draw needn't show every extreme that they name: `route_experts`: each row names 10 different experts. Within the 64 rows of one device (aligned blocks of 64 rows) no expert is named more than 6 times, and in every draw some device names some expert exactly 6 times.
All inputs are finite; a program needn't handle non-finite values.
Results may differ from the reference program's by a relative error of at most 0.02.
Values may be sent and summed in bfloat16 or wider, within the bound.
No kernel may reach another device: no remote copies, remote signals or barrier semaphores. Data moves between devices by JAX's collectives and lax.ppermute only.
A program may use at most 128 MiB of HBM per device.

```python
import math
import jax
import jax.numpy as jnp
import numpy as np
from jax import lax

D = 2048
KEY_HEADS = 16
VAL_HEADS = 32
HEAD_DIM = 128
KCONV = 4
FF = 512
TOPK = 10
BLOCK = 64
TOK_DEV = 256
KD = 2048
VD = 4096
TOKENS = 8192
MOE_ROWS = 64
EXPERTS = 256
CAP = 6
N_SEQ = 32
N_EXP = 4


def slow_heads(key):
    shuffled = jax.random.permutation(jax.random.fold_in(key, 101), VAL_HEADS)
    keeping = VAL_HEADS // 2
    return shuffled < keeping


def head_rates(key):
    slow = slow_heads(key)
    uniform_draw = jax.random.uniform(jax.random.fold_in(key, 102), (VAL_HEADS,), jnp.float32)
    slow_rate = (0.5 + uniform_draw) / TOKENS
    fast_rate = 0.03 + 0.03 * uniform_draw
    return jnp.where(slow, slow_rate, fast_rate)


def draw_decay_rate(key, part):
    return head_rates(key).astype(jnp.float32)


def draw_decay_logit(key, part):
    rates = head_rates(key)
    blocks = TOKENS // TOK_DEV
    offsets = jax.random.uniform(jax.random.fold_in(key, 103), (blocks, VAL_HEADS), jnp.float32, -1.0, 1.0)
    jitter = jnp.clip(jax.random.normal(jax.random.fold_in(key, 104), (TOKENS, VAL_HEADS), jnp.float32), -5.0, 5.0)
    starting_shift = jnp.repeat(offsets, TOK_DEV, axis=0) + jitter
    spots = jax.random.randint(jax.random.fold_in(key, 105), (4, VAL_HEADS), 0, TOKENS)
    kept = jax.random.uniform(jax.random.fold_in(key, 106), (4, VAL_HEADS), jnp.float32, 0.5, 0.8)
    target = -jnp.log(kept) / rates[None, :]
    reciprocal_operator = target + jnp.log(-jnp.expm1(-target))
    place_locator = jnp.arange(TOKENS)[:, None, None] == spots[None, :, :]
    dispatch_batch = jnp.sum(jnp.where(place_locator, reciprocal_operator[None, :, :], 0.0), axis=1)
    removed_elements = jnp.any(place_locator, axis=1)
    return jnp.where(removed_elements, dispatch_batch, starting_shift).astype(jnp.float32)


def draw_beta_logit(key, part):
    slow = slow_heads(key)
    center = jnp.where(slow, jnp.log(48.0 / TOKENS), 0.0)
    jitter = 0.5 * jnp.clip(jax.random.normal(jax.random.fold_in(key, 107), (TOKENS, VAL_HEADS), jnp.float32), -5.0, 5.0)
    return (center[None, :] + jitter).astype(jnp.float32)


def steps_of(key, dims, pieces, smallest, largest):
    level = 1.0
    for axis_at, parts in pieces:
        draws = jax.random.uniform(jax.random.fold_in(jax.random.fold_in(key, 6), axis_at), (parts,), jnp.float32, smallest / len(pieces), largest / len(pieces))
        level = level * jnp.repeat(jnp.exp(draws), dims[axis_at] // parts).reshape((-1,) + (1,) * (len(dims) - 1 - axis_at))
    return level


def shared_out(own_key, own, number, rows, count, top, limit, skew):
    order = jax.random.permutation(own_key, count)
    packed, ordinary = load_shares(count, rows * top, limit, skew, True), load_shares(count, rows * top, limit, skew, False)
    places = jnp.arange(count)

    def named(tallies, offset_by):
        used = int((tallies > 0).sum())
        fixed = max(1, used // 4)
        shifted = fixed + (places - fixed + offset_by * (used - fixed)) % max(1, count - fixed)
        return jnp.zeros((count,), jnp.int32).at[order[jnp.where(places < fixed, places, shifted)]].set(jnp.asarray(tallies, jnp.int32))

    tallies = jnp.where(number % 4 == 0, named(packed, number // 4), named(ordinary, number - number // 4 - 1))
    mixed = jax.random.permutation(jax.random.fold_in(own, 3), count)
    donor, receiver = mixed[0:count // 2 * 2:2], mixed[1:count // 2 * 2:2]
    margin = jnp.minimum(tallies[donor] - 1, limit - tallies[receiver]) // 2
    margin = jnp.where((donor == order[0]) | (receiver == order[0]) | (tallies[receiver] == 0), 0, jnp.maximum(margin, 0))
    shifted = jax.random.randint(jax.random.fold_in(own, 4), (count // 2,), 0, 1 << 20) % (margin + 1)
    tallies = tallies.at[donor].add(-shifted).at[receiver].add(shifted)
    items = jnp.searchsorted(jnp.cumsum(tallies), jnp.arange(rows * top), side="right").astype(jnp.int32)
    listing = items.reshape(top, rows).T
    listing = listing[jax.random.permutation(jax.random.fold_in(own, 1), rows)]
    offset_by = jax.random.randint(jax.random.fold_in(own, 2), (rows, 1), 0, top)
    return jnp.take_along_axis(listing, (jnp.arange(top)[None, :] + offset_by) % top, axis=1)


def load_shares(count, total, reach, skew, full):
    portions = [(1 << 20) // math.isqrt(grade ** skew) + 1 for grade in range(1, count + 1)]
    largest = reach if full else min(reach, max(-(-total // count), total * portions[0] // sum(portions)))
    least = 1 if total - largest >= count - 1 else 0
    holding, rest = [largest] + [least] * (count - 1), total - largest - least * (count - 1)
    while rest > 0:
        free = [i for i in range(1, count) if holding[i] < largest] or [i for i in range(1, count) if holding[i] < reach]
        mass, remaining = sum([portions[i] for i in free]), rest
        for i in free:
            extra = min(reach - holding[i], max(1, remaining * portions[i] // mass), rest)
            holding[i] = holding[i] + extra
            rest = rest - extra
    return np.array(holding)


def centred(key, extent, deviation, reach, pieces=(), held_as=jnp.bfloat16):
    drawn = jax.random.normal(key, extent, jnp.float32) * deviation
    if len(pieces) > 0:
        drawn = steps_of(key, extent, pieces, -0.22, 0.18) * drawn
    return jnp.clip(drawn, min=-reach, max=reach).astype(held_as)


def setup_inputs(seed: int = 0) -> dict:
    key_list = jax.random.split(jax.random.key(seed), 20)
    query_proj = centred(key_list[0], (TOKENS, KD), 1.0, 6.0, ((0, 32), (1, 4)))
    key_proj = centred(key_list[1], (TOKENS, KD), 1.0, 6.0, ((0, 32), (1, 4)))
    value_proj = centred(key_list[2], (TOKENS, VD), 1.0, 6.0, ((0, 32), (1, 4)))
    result_valve_maps = centred(key_list[3], (TOKENS, VD), 1.0, 6.0, ((0, 32), (1, 4)))
    beta_logit = draw_beta_logit(jax.random.fold_in(key_list[19], 71), 0)
    decay_logit = draw_decay_logit(jax.random.fold_in(key_list[19], 71), 0)
    decay_rate = draw_decay_rate(jax.random.fold_in(key_list[19], 71), 0)
    conv_query = centred(key_list[7], (KCONV, KD), KCONV ** -0.5, 3.0, ((1, 4),), jnp.float32)
    conv_key = centred(key_list[8], (KCONV, KD), KCONV ** -0.5, 3.0, ((1, 4),), jnp.float32)
    conv_value = centred(key_list[9], (KCONV, VD), KCONV ** -0.5, 3.0, ((1, 4),), jnp.float32)
    norm_gain = jnp.clip(1.0 + 0.18 * jax.random.normal(key_list[10], (HEAD_DIM,), jnp.float32), 0.1, 1.9)
    output_weight = centred(key_list[11], (VD, D), VD ** -0.5, 0.09375, ((0, 4),))
    residual = centred(key_list[12], (TOKENS, D), 1.0, 6.0, ((0, 128),))
    post_gain = jnp.clip(1.0 + 0.18 * jax.random.normal(key_list[13], (D,), jnp.float32), 0.1, 1.9)
    route_experts_keys = jax.random.split(jax.random.fold_in(key_list[14], 1), TOKENS // MOE_ROWS)
    route_experts_turns = jax.random.permutation(jax.random.fold_in(key_list[14], 3), TOKENS // MOE_ROWS)
    route_experts = jax.vmap(lambda own, number: shared_out(jax.random.fold_in(key_list[14], 2), own, number, MOE_ROWS, EXPERTS, TOPK, CAP, 2))(route_experts_keys, route_experts_turns).reshape((TOKENS, TOPK))
    route_weights = jnp.clip(jnp.exp(math.log(1.0) - 2.9957323 * jax.random.uniform(key_list[15], (TOKENS, TOPK), jnp.float32) ** steps_of(key_list[15], (TOKENS, TOPK), ((0, 128),), -0.2, 0.2)), 0.05, 1.0)
    expert_gate = centred(key_list[16], (EXPERTS, D, FF), D ** -0.5, 0.125, ((0, 128),))
    expert_up = centred(key_list[17], (EXPERTS, D, FF), D ** -0.5, 0.125, ((0, 128),))
    expert_down = centred(key_list[18], (EXPERTS, FF, D), FF ** -0.5, 0.25, ((0, 128),))
    return {"query_proj": query_proj, "key_proj": key_proj, "value_proj": value_proj, "result_valve_maps": result_valve_maps, "beta_logit": beta_logit, "decay_logit": decay_logit, "decay_rate": decay_rate, "conv_query": conv_query, "conv_key": conv_key, "conv_value": conv_value, "norm_gain": norm_gain, "output_weight": output_weight, "residual": residual, "post_gain": post_gain, "route_experts": route_experts, "route_weights": route_weights, "expert_gate": expert_gate, "expert_up": expert_up, "expert_down": expert_down}


highest = lax.Precision.HIGHEST
epsilon = 1e-06

def causal_conv(value_rows, kernel, leading):
    padded = jnp.concatenate([leading, value_rows], axis=0)
    length = value_rows.shape[0]
    running = jnp.zeros_like(value_rows)
    for offset in range(kernel.shape[0]):
        running = running + kernel[offset] * padded[offset:offset + length]
    return jax.nn.silu(running)

def block_terms(queries, key_rows, value_rows, beta_gate, log_decay):
    block_size = queries.shape[-2]
    cumulative = jnp.cumsum(log_decay, axis=-1)
    spread = cumulative[..., :, None] - cumulative[..., None, :]
    row_index = lax.broadcasted_iota(jnp.int32, (block_size, block_size), 0)
    col_index = lax.broadcasted_iota(jnp.int32, (block_size, block_size), 1)
    lower_mask = row_index >= col_index
    strict = row_index > col_index
    decay_mask = jnp.where(lower_mask, jnp.exp(jnp.where(lower_mask, spread, 0.0)), 0.0)
    key_key = jnp.einsum('...id,...jd->...ij', key_rows, key_rows, precision=highest)
    coupling = jnp.where(strict, beta_gate[..., :, None] * key_key * decay_mask, 0.0)
    identity = jnp.eye(block_size, dtype=jnp.float32)
    growth = jnp.exp(cumulative)
    stacked = jnp.concatenate([beta_gate[..., None] * value_rows, (beta_gate * growth)[..., None] * key_rows], axis=-1)
    solved = jax.scipy.linalg.solve_triangular(identity + coupling, stacked, lower=True, unit_diagonal=True)
    payload_width = value_rows.shape[-1]
    updates = solved[..., :payload_width]
    key_mix = solved[..., payload_width:]
    scores = jnp.einsum('...id,...jd->...ij', queries, key_rows, precision=highest) * decay_mask
    local_out = jnp.einsum('...ij,...jv->...iv', scores, updates, precision=highest)
    lifted = growth[..., None] * queries - jnp.einsum('...ij,...jd->...id', scores, key_mix, precision=highest)
    remain = jnp.exp(cumulative[..., -1:] - cumulative)
    key_tail = key_rows * remain[..., None]
    key_dim = key_rows.shape[-1]
    carry_map = jnp.exp(cumulative[..., -1])[..., None, None] * jnp.eye(key_dim, dtype=jnp.float32) - jnp.einsum('...ci,...cj->...ij', key_mix, key_tail, precision=highest)
    write_term = jnp.einsum('...cv,...ck->...vk', updates, key_tail, precision=highest)
    return (local_out, lifted, carry_map, write_term)

def head_chain(head_inputs):
    queries, key_rows, value_rows, beta_gate, log_decay = head_inputs
    local_out, lifted, carry_map, write_term = block_terms(queries, key_rows, value_rows, beta_gate, log_decay)

    def advance(memory, block_item):
        block_out, block_lift, block_map, block_write = block_item
        result = block_out + jnp.einsum('cd,vd->cv', block_lift, memory, precision=highest)
        memory = jnp.einsum('vd,de->ve', memory, block_map, precision=highest) + block_write
        return (memory, result)
    initial = jnp.zeros((value_rows.shape[-1], key_rows.shape[-1]), jnp.float32)
    _, outputs = lax.scan(advance, initial, (local_out, lifted, carry_map, write_term))
    return outputs

def reference(query_proj, key_proj, value_proj, result_valve_maps, beta_logit, decay_logit, decay_rate, conv_query, conv_key, conv_value, norm_gain, output_weight, residual, post_gain, route_experts, route_weights, expert_gate, expert_up, expert_down):
    rim_width = KCONV - 1
    query_conv = causal_conv(query_proj.astype(jnp.float32), conv_query, jnp.zeros((rim_width, KD), jnp.float32))
    key_conv = causal_conv(key_proj.astype(jnp.float32), conv_key, jnp.zeros((rim_width, KD), jnp.float32))
    value_conv = causal_conv(value_proj.astype(jnp.float32), conv_value, jnp.zeros((rim_width, VD), jnp.float32))
    key_split = key_conv.reshape(TOKENS, KEY_HEADS, HEAD_DIM)
    key_unit = key_split * lax.rsqrt(lax.optimization_barrier(jnp.sum(key_split * key_split, axis=-1, keepdims=True)) + epsilon)
    query_rep = jnp.repeat(query_conv.reshape(TOKENS, KEY_HEADS, HEAD_DIM), 2, axis=1)
    key_rep = jnp.repeat(key_unit, 2, axis=1)
    value_split = value_conv.reshape(TOKENS, VAL_HEADS, HEAD_DIM)
    beta_gate = jax.nn.sigmoid(beta_logit)
    log_decay = -decay_rate[None, :] * jax.nn.softplus(decay_logit)
    blocks = TOKENS // BLOCK

    def arrange(array):
        return array.reshape(blocks, BLOCK, VAL_HEADS, HEAD_DIM).transpose(2, 0, 1, 3)

    def arrange_gate(array):
        return array.reshape(blocks, BLOCK, VAL_HEADS).transpose(2, 0, 1)
    core = lax.map(head_chain, (arrange(query_rep), arrange(key_rep), arrange(value_split), arrange_gate(beta_gate), arrange_gate(log_decay)))
    core = core.transpose(1, 2, 0, 3).reshape(TOKENS, VAL_HEADS, HEAD_DIM)
    gate_heads = result_valve_maps.astype(jnp.float32).reshape(TOKENS, VAL_HEADS, HEAD_DIM)
    mean_square = lax.optimization_barrier(jnp.mean(core * core, axis=-1, keepdims=True))
    normed = (core * lax.rsqrt(mean_square + epsilon) * norm_gain * jax.nn.silu(gate_heads)).astype(jnp.bfloat16).reshape(TOKENS, VD)
    mixer = jnp.dot(normed.astype(jnp.float32), output_weight.astype(jnp.float32), preferred_element_type=jnp.float32)
    mixer_out = (residual.astype(jnp.float32) + mixer).astype(jnp.bfloat16)
    mixed = mixer_out.astype(jnp.float32)
    moe_in = (mixed * lax.rsqrt(lax.optimization_barrier(jnp.mean(mixed * mixed, axis=-1, keepdims=True)) + epsilon) * post_gain).astype(jnp.bfloat16)
    shares = route_weights / lax.optimization_barrier(jnp.sum(route_weights, axis=1, keepdims=True))
    linear_labels = route_experts.reshape(-1).astype(jnp.int32)
    flat_shares = shares.reshape(-1)
    pick_order = jnp.argsort(linear_labels, stable=True).astype(jnp.int32)
    counts = jax.ops.segment_sum(jnp.ones_like(linear_labels), linear_labels, num_segments=EXPERTS).astype(jnp.int32)
    starts = (jnp.cumsum(counts) - counts).astype(jnp.int32)
    window = CAP * N_SEQ * N_EXP
    order_padded = jnp.concatenate([pick_order, jnp.zeros((window,), jnp.int32)])

    def add_expert(summed_total, expert_item):
        gate_matrix, up_matrix, down_matrix, expert = expert_item
        picked = lax.dynamic_slice(order_padded, (starts[expert].astype(jnp.int32),), (window,))
        live_mask = jnp.arange(window, dtype=jnp.int32) < counts[expert]
        token_rows = (picked // TOPK).astype(jnp.int32)
        inputs = moe_in[token_rows]
        gate_act = jnp.dot(inputs.astype(jnp.float32), gate_matrix.astype(jnp.float32), preferred_element_type=jnp.float32)
        up_act = jnp.dot(inputs.astype(jnp.float32), up_matrix.astype(jnp.float32), preferred_element_type=jnp.float32)
        inner = (jax.nn.silu(gate_act) * up_act).astype(jnp.bfloat16)
        expert_res = jnp.dot(inner.astype(jnp.float32), down_matrix.astype(jnp.float32), preferred_element_type=jnp.float32).astype(jnp.bfloat16)
        contrib = jnp.where(live_mask[:, None], flat_shares[picked][:, None] * expert_res.astype(jnp.float32), 0.0)
        return (summed_total.at[token_rows].add(contrib), None)
    summed_total, _ = lax.scan(add_expert, jnp.zeros((TOKENS, D), jnp.float32), (expert_gate, expert_up, expert_down, jnp.arange(EXPERTS, dtype=jnp.int32)))
    expert_mixture = summed_total.astype(jnp.bfloat16)
    return (mixer_out, expert_mixture)
```

```python
import jax
import jax.numpy as jnp
from jax import lax
from jax.experimental import pallas as pl
from jax.experimental.pallas import tpu as pltpu
from jax.sharding import PartitionSpec as P

f32 = jnp.float32
bf16 = jnp.bfloat16
EPS = 1e-06
HD = 128
BLK = 128
TOK = 256
HALO = 8
SEQ = 32
NEAR = 8
FAR = SEQ // NEAR
EXP = 4
DEV = SEQ * EXP
ROWS = 64
PICKS = 10
CAP = 6
NQ = 4
CH = 2 * CAP * NQ
QW = 512
FF = 512
VMEM = 56 * 1024 * 1024


def iota(shape, dim):
    return lax.broadcasted_iota(jnp.int32, shape, dim)


def split(a):
    hi = a.astype(bf16)
    return hi, (a - hi.astype(f32)).astype(bf16)


def dot(a, b, dims=((1,), (0,))):
    return lax.dot_general(a, b, (dims, ((), ())), preferred_element_type=f32)


def dot3(a, b, dims=((1,), (0,))):
    return dot(a[0], b[0], dims) + (dot(a[0], b[1], dims) + dot(a[1], b[0], dims))


NT = ((1,), (1,))
TN = ((0,), (0,))


def conv_silu(ref, halo_ref, taps_ref, pad_ref):
    width = ref.shape[1]
    pad_ref[0:HALO, 0:width] = halo_ref[...].astype(f32)
    pad_ref[HALO : HALO + TOK, 0:width] = ref[...].astype(f32)
    run = taps_ref[0:1, :] * pad_ref[HALO - 3 : HALO - 3 + TOK, 0:width]
    for j in range(1, 4):
        run = run + taps_ref[j : j + 1, :] * pad_ref[HALO - 3 + j : HALO - 3 + j + TOK, 0:width]
    return run / (1.0 + jnp.exp(-run))


def odd_rows(x, size):
    return jnp.concatenate(
        [x[m * size : (m + 1) * size] for m in range(1, BLK // size, 2)], axis=0
    )


def inverses(couplings):
    count = len(couplings)
    lane = iota((8, BLK), 1)
    sub = iota((8, BLK), 0)
    slabs = [[] for _ in range(count)]
    for m in range(BLK // 8):
        a = [c[8 * m : 8 * m + 8] for c in couplings]
        t = [(lane == sub + 8 * m).astype(f32)] * count
        for j in range(7):
            t = [t[n] - a[n][:, 8 * m + j : 8 * m + j + 1] * t[n][j : j + 1, :] for n in range(count)]
        for n in range(count):
            slabs[n].append(t[n])
    ts = [jnp.concatenate(x, axis=0) for x in slabs]
    half = BLK // 2
    rows = iota((half, BLK), 0)
    cols = iota((half, BLK), 1)
    size = 8
    while size < BLK:
        part = cols // size == 2 * (rows // size)
        zero = jnp.zeros((size, BLK), f32)
        prods = [
            dot3(split(jnp.where(part, odd_rows(c, size), 0.0)), split(t)) for c, t in zip(couplings, ts)
        ]
        lowers = []
        for prod, t in zip(prods, ts):
            tall = []
            for m in range(half // size):
                tall += [zero, prod[m * size : (m + 1) * size]]
            lower = odd_rows(t, size)
            lowers.append(lower - dot3(split(lower), split(jnp.concatenate(tall, axis=0))))
        new = []
        for lower, t in zip(lowers, ts):
            pieces = []
            for m in range(half // size):
                pieces += [t[2 * m * size : (2 * m + 1) * size], lower[m * size : (m + 1) * size]]
            new.append(jnp.concatenate(pieces, axis=0))
        ts = new
        size *= 2
    return [split(t) for t in ts]


def mixer_body(q_ref, k_ref, v_ref, hq_ref, hk_ref, hv_ref, bl_ref, dl_ref, rate_ref, cq_ref, ck_ref, cv_ref,
               map_ref, local_ref, lift_ref, pad_ref, cum_ref, beta_ref):
    step = pl.program_id(0)
    row = iota((BLK, BLK), 0)
    col = iota((BLK, BLK), 1)
    x = dl_ref[...]
    soft = jnp.maximum(x, 0.0) + jnp.log1p(jnp.exp(-jnp.abs(x)))
    decay = jnp.maximum(-rate_ref[...] * soft, -110.0)
    upper = (row <= col).astype(f32)
    for b in range(2):
        cum_ref[b] = lax.dot_general(decay[:, b * BLK : (b + 1) * BLK], upper, (((1,), (0,)), ((), ())),
                                     precision=lax.Precision.HIGHEST, preferred_element_type=f32)
        beta_ref[b] = 1.0 / (1.0 + jnp.exp(-bl_ref[:, b * BLK : (b + 1) * BLK]))

    queries = conv_silu(q_ref, hq_ref, cq_ref, pad_ref)
    keys = conv_silu(k_ref, hk_ref, ck_ref, pad_ref)
    keys = keys * lax.rsqrt(jnp.sum(keys * keys, axis=1, keepdims=True) + EPS)
    values = conv_silu(v_ref, hv_ref, cv_ref, pad_ref)

    rows = []
    for b in range(2):
        for i in range(2):
            rows.append(cum_ref[b, pl.ds(2 * step + i, 1), :])
            rows.append(beta_ref[b, pl.ds(2 * step + i, 1), :])
    wide = jnp.concatenate(rows + [jnp.zeros((BLK - 8, BLK), f32)], axis=0)
    tall = wide.T

    res = {}
    keyed = [(b, i) for b in range(2) for i in range(2)]
    grams, scores, masks, couplings = {}, {}, {}, []
    for b in range(2):
        kb = split(keys[b * BLK : (b + 1) * BLK])
        grams[b] = dot3(kb, kb, NT)
        scores[b] = dot(queries[b * BLK : (b + 1) * BLK].astype(bf16), kb[0], NT)
    for b, i in keyed:
        at = 2 * (2 * b + i)
        spread = tall[:, at : at + 1] - rows[at]
        masks[b, i] = jnp.where(row >= col, jnp.exp(jnp.where(row >= col, spread, 0.0)), 0.0)
        couplings.append(jnp.where(row > col, tall[:, at + 1 : at + 2] * grams[b] * masks[b, i], 0.0))
    invs = dict(zip(keyed, inverses(couplings)))
    for b, i in keyed:
        at = 2 * (2 * b + i)
        cum_c = tall[:, at : at + 1]
        beta_c = tall[:, at + 1 : at + 2]
        qb = queries[b * BLK : (b + 1) * BLK]
        kb = keys[b * BLK : (b + 1) * BLK]
        vb = values[b * BLK : (b + 1) * BLK, i * HD : (i + 1) * HD]
        grow = jnp.exp(cum_c)
        last = cum_c[BLK - 1 : BLK, :]
        key_tail = (kb * jnp.exp(last - cum_c)).astype(bf16)
        rhs = jnp.concatenate([beta_c * vb, (beta_c * grow) * kb], axis=1)
        solved = dot3(invs[b, i], split(rhs)).astype(bf16)
        near = dot((scores[b] * masks[b, i]).astype(bf16), solved)
        local = near[:, :HD]
        lift = grow * qb - near[:, HD:]
        both = dot(solved, key_tail, TN)
        res[b, i] = (local, lift, jnp.exp(last), both)
    for i in range(2):
        l0, f0, t0, both0 = res[0, i]
        l1, f1, t1, both1 = res[1, i]
        w0, gone0 = both0[:HD], both0[HD:]
        w1, gone1 = both1[:HD], both1[HD:]
        first = both0.astype(bf16)
        joined = dot(first, gone1.astype(bf16))
        w = t1 * w0 - joined[:HD] + w1
        m = (t0 * t1) * (row == col).astype(f32) - t0 * gone1 - t1 * gone0 + joined[HD:]
        moved = dot(f1.astype(bf16), first, NT)
        local_ref[i, 0:BLK] = l0
        local_ref[i, BLK:TOK] = l1 + moved[:, :HD]
        lift_ref[i, 0:BLK] = f0.astype(bf16)
        lift_ref[i, BLK:TOK] = (t0 * f1 - moved[:, HD:]).astype(bf16)
        map_ref[i, 0:HD] = m.astype(bf16)
        map_ref[i, HD : 2 * HD] = w.astype(bf16)


def mixer_blocks(q, k, v, halo, beta_t, decay_t, rate, cq, ck, cv):
    w = HD
    return pl.pallas_call(
        mixer_body,
        grid=(4,),
        in_specs=[
            pl.BlockSpec((TOK, w), lambda s: (0, s)),
            pl.BlockSpec((TOK, w), lambda s: (0, s)),
            pl.BlockSpec((TOK, 2 * w), lambda s: (0, s)),
            pl.BlockSpec((HALO, w), lambda s: (0, s)),
            pl.BlockSpec((HALO, w), lambda s: (0, 4 + s)),
            pl.BlockSpec((HALO, 2 * w), lambda s: (0, 4 + s)),
            pl.BlockSpec((8, TOK), lambda s: (0, 0)),
            pl.BlockSpec((8, TOK), lambda s: (0, 0)),
            pl.BlockSpec((8, 1), lambda s: (0, 0)),
            pl.BlockSpec((4, w), lambda s: (0, s)),
            pl.BlockSpec((4, w), lambda s: (0, s)),
            pl.BlockSpec((4, 2 * w), lambda s: (0, s)),
        ],
        out_specs=[
            pl.BlockSpec((2, 2 * HD, HD), lambda s: (s, 0, 0)),
            pl.BlockSpec((2, TOK, HD), lambda s: (s, 0, 0)),
            pl.BlockSpec((2, TOK, HD), lambda s: (s, 0, 0)),
        ],
        out_shape=[
            jax.ShapeDtypeStruct((NEAR, 2 * HD, HD), bf16),
            jax.ShapeDtypeStruct((8, TOK, HD), f32),
            jax.ShapeDtypeStruct((8, TOK, HD), bf16),
        ],
        scratch_shapes=[
            pltpu.VMEM((TOK + HALO, 2 * HD), f32),
            pltpu.VMEM((2, 8, BLK), f32),
            pltpu.VMEM((2, 8, BLK), f32),
        ],
        compiler_params=pltpu.CompilerParams(vmem_limit_bytes=VMEM),
        name="mixer_blocks",
    )(q, k, v, halo, halo, halo, beta_t, decay_t, rate, cq, ck, cv)


def in_vmem(count):
    return [pl.BlockSpec(memory_space=pltpu.VMEM)] * count


def vmem(mib):
    return pltpu.CompilerParams(vmem_limit_bytes=mib * 1024 * 1024)


def near_body(in_ref, map_ref, mem_ref, all_ref):
    both = in_ref[0].astype(f32)
    for j in range(1, NEAR):
        hi, lo = split(both)
        map_ref[j - 1] = hi[:HD]
        mem_ref[j - 1] = both[HD:]
        here = in_ref[j]
        both = dot(hi, here[:HD]) + dot(lo, here[:HD])
        both = jnp.concatenate([both[:HD], both[HD:] + here[HD:].astype(f32)], axis=0)
    for g in range(FAR):
        all_ref[g] = both.astype(bf16)


def near_scan(maps):
    return pl.pallas_call(
        near_body,
        in_specs=in_vmem(1),
        out_shape=[
            jax.ShapeDtypeStruct((NEAR - 1, HD, HD), bf16),
            jax.ShapeDtypeStruct((NEAR - 1, HD, HD), f32),
            jax.ShapeDtypeStruct((FAR, 2 * HD, HD), bf16),
        ],
        compiler_params=vmem(8),
        name="near_scan",
    )(maps)


def far_body(at_ref, all_ref, map_ref, mem_ref, out_ref):
    state = jnp.zeros((HD, HD), f32)
    entry = state
    for g in range(FAR - 1):
        if g == 0:
            state = all_ref[0, HD:].astype(f32)
        else:
            hi, lo = split(state)
            here = all_ref[g]
            state = dot(hi, here[:HD]) + dot(lo, here[:HD]) + here[HD:].astype(f32)
        entry = jnp.where(at_ref[0] == g + 1, state, entry)
    hi, lo = split(entry)
    out_ref[0] = hi
    for j in range(1, NEAR):
        m = map_ref[j - 1]
        out_ref[j] = (dot(hi, m) + dot(lo, m) + mem_ref[j - 1]).astype(bf16)


def far_scan(place, totals, maps, memories):
    return pl.pallas_call(
        far_body,
        in_specs=[pl.BlockSpec(memory_space=pltpu.SMEM)] + in_vmem(3),
        out_shape=jax.ShapeDtypeStruct((NEAR, HD, HD), bf16),
        compiler_params=vmem(8),
        name="far_scan",
    )(place, totals, maps, memories)


def project_body(s_ref, local_ref, lift_ref, gate_ref, gain_ref, w_ref, out_ref, norm_ref):
    for h in range(8):
        core = local_ref[h] + dot(lift_ref[h], s_ref[h], NT)
        gate = gate_ref[:, h * HD : (h + 1) * HD].astype(f32)
        ms = jnp.sum(core * core, axis=1, keepdims=True) * (1.0 / HD)
        act = gate / (1.0 + jnp.exp(-gate))
        norm_ref[:, h * HD : (h + 1) * HD] = (core * lax.rsqrt(ms + EPS) * gain_ref[...] * act).astype(bf16)
    for n in range(4):
        out = dot(norm_ref[...], w_ref[:, n * QW : (n + 1) * QW]).astype(bf16)
        for e in range(EXP):
            out_ref[e, :, n * QW : (n + 1) * QW] = out[e * ROWS : (e + 1) * ROWS]


def project(states, local, lift, gate, gain, weight):
    return pl.pallas_call(
        project_body,
        in_specs=in_vmem(6),
        out_shape=jax.ShapeDtypeStruct((EXP, ROWS, 2048), bf16),
        scratch_shapes=[pltpu.VMEM((TOK, 8 * HD), bf16)],
        compiler_params=vmem(16),
        name="project",
    )(states, local, lift, gate, gain, weight)


def route_body(experts_ref, weights_ref, pick_ref, part_ref, slot_ref, share_ref):
    ids = experts_ref[...]
    weights = weights_ref[...]
    shares = weights / jnp.sum(weights, axis=1, keepdims=True)
    lane = iota((ROWS, DEV), 1)
    token = iota((ROWS, DEV), 0).astype(f32)
    earlier = (iota((ROWS, ROWS), 0) > iota((ROWS, ROWS), 1)).astype(bf16)
    for e in range(2):
        named = jnp.zeros((ROWS, DEV), f32)
        part = jnp.zeros((ROWS, DEV), f32)
        for k in range(PICKS):
            hit = ids[:, k : k + 1] == 2 * lane + e
            named = named + jnp.where(hit, 1.0, 0.0)
            part = part + jnp.where(hit, shares[:, k : k + 1], 0.0)
        rank = dot(earlier, named.astype(bf16))
        for r in range(CAP):
            hit = (named > 0.5) & (rank == float(r))
            used = jnp.sum(jnp.where(hit, 1.0, 0.0), axis=0, keepdims=True)
            tok = jnp.sum(jnp.where(hit, token, 0.0), axis=0, keepdims=True)
            share = jnp.sum(jnp.where(hit, part, 0.0), axis=0, keepdims=True)
            for q in range(NQ):
                j = q * 2 * CAP + e * CAP + r
                slot_ref[j : j + 1, :] = jnp.where(used > 0.5, tok + float(ROWS * q), -1.0)
                share_ref[j : j + 1, :] = share
    slots = slot_ref[...]
    shs = share_ref[...]
    lane2 = iota((CH, NQ * ROWS), 1).astype(f32)
    for g in range(DEV // 8):
        tall = []
        for d in range(8 * g, 8 * g + 8):
            hit = slots[:, d : d + 1] == lane2
            pick_ref[d * CH : (d + 1) * CH, :] = jnp.where(hit, 1.0, 0.0).astype(bf16)
            tall.append(jnp.where(hit, shs[:, d : d + 1], 0.0))
        part_ref[:, g * 8 * CH : (g + 1) * 8 * CH] = jnp.concatenate(tall, axis=0).T.astype(bf16)


def route(experts, weights):
    return pl.pallas_call(
        route_body,
        out_shape=[
            jax.ShapeDtypeStruct((DEV * CH, NQ * ROWS), bf16),
            jax.ShapeDtypeStruct((NQ * ROWS, DEV * CH), bf16),
        ],
        scratch_shapes=[pltpu.VMEM((CH, DEV), f32), pltpu.VMEM((CH, DEV), f32)],
        compiler_params=vmem(16),
        name="route",
    )(experts, weights)


def dispatch_body(parts_ref, res_ref, gain_ref, pick_ref, mix_ref, out_ref, stack_ref):
    total = parts_ref[0].astype(f32)
    for e in range(1, EXP):
        total = total + parts_ref[e].astype(f32)
    mixed = (res_ref[...].astype(f32) + total).astype(bf16)
    mix_ref[...] = mixed
    m = mixed.astype(f32)
    ms = jnp.sum(m * m, axis=1, keepdims=True) * (1.0 / (NQ * QW))
    normed = (m * lax.rsqrt(ms + EPS) * gain_ref[...]).astype(bf16)
    for q in range(NQ):
        stack_ref[q * ROWS : (q + 1) * ROWS, :] = normed[:, q * QW : (q + 1) * QW]
    step = DEV * CH // 8
    for n in range(8):
        out_ref[n * step : (n + 1) * step, :] = dot(
            pick_ref[n * step : (n + 1) * step, :], stack_ref[...]
        ).astype(bf16)


def dispatch(parts, residual, gain, pick):
    return pl.pallas_call(
        dispatch_body,
        in_specs=in_vmem(4),
        out_shape=[
            jax.ShapeDtypeStruct((ROWS, 2048), bf16),
            jax.ShapeDtypeStruct((DEV * CH, QW), bf16),
        ],
        scratch_shapes=[pltpu.VMEM((NQ * ROWS, QW), bf16)],
        compiler_params=vmem(16),
        name="dispatch",
    )(parts, residual, gain, pick)


GS = 4
GR = GS * CH
PR = GS * CAP


def expert_body(in_ref, gate_ref, up_ref, down_ref, out_ref, x_ref, y_ref):
    def place(n):
        rest = n % CH
        return (rest // CAP) * PR + (n // CH) * CAP + rest % CAP

    perm = (iota((GR, GR), 0) == place(iota((GR, GR), 1))).astype(bf16)
    perm_t = (iota((GR, GR), 1) == place(iota((GR, GR), 0))).astype(bf16)
    pairs = DEV // (2 * GS)

    def load(i, _):
        a = dot(perm, in_ref[pl.ds(2 * GR * i, GR), :])
        b = dot(perm, in_ref[pl.ds(2 * GR * i + GR, GR), :])
        for q in range(NQ):
            for e in range(2):
                at = (2 * q + e) * PR
                both = jnp.concatenate([a[at : at + PR], b[at : at + PR]], axis=0).astype(bf16)
                x_ref[e, pl.ds(2 * PR * i, 2 * PR), q * QW : (q + 1) * QW] = both
        return 0

    lax.fori_loop(0, pairs, load, 0, unroll=2)
    for e in range(2):
        x = x_ref[e]
        g = dot(x, gate_ref[e])
        u = dot(x, up_ref[e])
        inner = (g / (1.0 + jnp.exp(-g)) * u).astype(bf16)
        y_ref[e] = dot(inner, down_ref[e]).astype(bf16)

    def store(i, _):
        halves = ([], [])
        for q in range(NQ):
            for e in range(2):
                both = y_ref[e, pl.ds(2 * PR * i, 2 * PR), q * QW : (q + 1) * QW].astype(f32)
                halves[0].append(both[:PR])
                halves[1].append(both[PR:])
        for h in range(2):
            z = jnp.concatenate(halves[h], axis=0).astype(bf16)
            out_ref[pl.ds(2 * GR * i + GR * h, GR), :] = dot(perm_t, z).astype(bf16)
        return 0

    lax.fori_loop(0, pairs, store, 0, unroll=2)


def experts_mlp(arrived, gate, up, down):
    return pl.pallas_call(
        expert_body,
        in_specs=in_vmem(4),
        out_shape=jax.ShapeDtypeStruct((DEV * CH, QW), bf16),
        scratch_shapes=[
            pltpu.VMEM((2, DEV * CAP, 2048), bf16),
            pltpu.VMEM((2, DEV * CAP, 2048), bf16),
        ],
        compiler_params=vmem(26),
        name="experts_mlp",
    )(arrived, gate, up, down)


def combine_body(part_ref, back_ref, out_ref):
    acc = dot(part_ref[...], back_ref[...])
    for q in range(NQ):
        out_ref[:, q * QW : (q + 1) * QW] = acc[q * ROWS : (q + 1) * ROWS, :].astype(bf16)


def combine(part, back):
    return pl.pallas_call(
        combine_body,
        in_specs=in_vmem(2),
        out_shape=jax.ShapeDtypeStruct((ROWS, 2048), bf16),
        compiler_params=vmem(8),
        name="combine",
    )(part, back)


def exchange(rows):
    chunks = rows.reshape(DEV, CH, QW)
    moved = lax.all_to_all(chunks, ("seq", "exp"), split_axis=0, concat_axis=0, tiled=True)
    return moved.reshape(DEV * CH, QW)


def body(
    query_proj,
    key_proj,
    value_proj,
    result_valve_maps,
    beta_logit,
    decay_logit,
    decay_rate,
    conv_query,
    conv_key,
    conv_value,
    norm_gain,
    output_weight,
    residual,
    post_gain,
    route_experts,
    route_weights,
    expert_gate,
    expert_up,
    expert_down,
):
    edge = jnp.concatenate(
        [a[TOK - HALO :] for a in (query_proj, key_proj, value_proj)], axis=1
    )
    halo = lax.ppermute(edge, "seq", [(s, s + 1) for s in range(SEQ - 1)])
    pick, share = route(route_experts, route_weights)
    maps, local, lift = mixer_blocks(
        query_proj,
        key_proj,
        value_proj,
        halo,
        beta_logit.T,
        decay_logit.T,
        decay_rate[:, None],
        conv_query,
        conv_key,
        conv_value,
    )
    near = [[g * NEAR + j for j in range(NEAR)] for g in range(FAR)]
    far = [[g * NEAR + j for g in range(FAR)] for j in range(NEAR)]

    def swap(array, groups):
        return lax.all_to_all(array, "seq", split_axis=0, concat_axis=0, axis_index_groups=groups, tiled=True)

    before, memories, totals = near_scan(swap(maps, near))
    place = (lax.axis_index("seq") // NEAR).astype(jnp.int32).reshape(1)
    states = swap(far_scan(place, swap(totals, far), before, memories), near)
    parts = project(
        states, local, lift, result_valve_maps, norm_gain[None, :], output_weight
    )
    parts = lax.all_to_all(parts, "exp", split_axis=0, concat_axis=0, tiled=True)
    mixer_out, outgoing = dispatch(parts, residual, post_gain[None, :], pick)
    finished = experts_mlp(exchange(outgoing), expert_gate, expert_up, expert_down)
    return (mixer_out, combine(share, exchange(finished)))


def solution(mesh):
    wide = P("seq", "exp")
    rows = P(("seq", "exp"), None)
    whole = P(("seq", "exp"), None, None)
    taps = P(None, "exp")
    in_specs = (wide, wide, wide, wide, wide, wide, P("exp"), taps, taps, taps, P(), P("exp", None), rows, P(), rows, rows, whole, whole, whole)
    return jax.shard_map(body, mesh=mesh, in_specs=in_specs, out_specs=(rows, rows), check_vma=False)
```

```python
import jax
import jax.numpy as jnp
from jax import lax
from jax.experimental import pallas as pl
from jax.experimental.pallas import tpu as pltpu
from jax.sharding import PartitionSpec as P

f32 = jnp.float32
bf16 = jnp.bfloat16
EPS = 1e-06
HD = 128
BLK = 128
SUB = 16
KH = 2
TOK = 256
HALO = 8
SEQ = 32
NEAR = 8
FAR = SEQ // NEAR
EXP = 4
DEV = SEQ * EXP
ROWS = 64
PICKS = 10
CAP = 6
NQ = 4
CH = 2 * CAP * NQ
QW = 512
FF = 512
VMEM = 56 * 1024 * 1024


def iota(shape, dim):
    return lax.broadcasted_iota(jnp.int32, shape, dim)


def split(a):
    hi = a.astype(bf16)
    return hi, (a - hi.astype(f32)).astype(bf16)


def dot(a, b, dims=((1,), (0,))):
    return lax.dot_general(a, b, (dims, ((), ())), preferred_element_type=f32)


def dot3(a, b, dims=((1,), (0,))):
    return dot(a[0], b[0], dims) + (dot(a[0], b[1], dims) + dot(a[1], b[0], dims))


NT = ((1,), (1,))
TN = ((0,), (0,))


def conv_silu(ref, halo, taps_ref, pad_ref):
    width = ref.shape[1]
    pad_ref[0:HALO, 0:width] = halo.astype(f32)
    pad_ref[HALO : HALO + TOK, 0:width] = ref[...].astype(f32)
    run = taps_ref[0:1, :] * pad_ref[HALO - 3 : HALO - 3 + TOK, 0:width]
    for j in range(1, 4):
        run = run + taps_ref[j : j + 1, :] * pad_ref[HALO - 3 + j : HALO - 3 + j + TOK, 0:width]
    return run / (1.0 + jnp.exp(-run))


def odd_rows(x, size):
    return jnp.concatenate(
        [x[m * size : (m + 1) * size] for m in range(1, BLK // size, 2)], axis=0
    )


def fill_spread(ref):
    width = (SUB - 1) * BLK
    src = iota((BLK, width), 0)
    dst = iota((BLK, width), 1)
    ref[...] = (src == SUB * ((dst % BLK) // SUB) + dst // BLK).astype(bf16)


def inverses(couplings, spread_ref):
    count = len(couplings)
    lane = iota((SUB, BLK), 1)
    sub = iota((SUB, BLK), 0)
    packs = []
    for c in couplings:
        pack = jnp.zeros((SUB, BLK), f32)
        for m in range(BLK // SUB):
            pack = jnp.where(lane // SUB == m, c[SUB * m : SUB * (m + 1)], pack)
        packs.append(pack)
    hi, lo = split(jnp.concatenate(packs, axis=0))
    small = [(lane % SUB == sub).astype(f32)] * count
    for j in range(SUB - 1):
        span = slice(j * BLK, (j + 1) * BLK)
        wide = dot(hi, spread_ref[:, span]) + dot(lo, spread_ref[:, span])
        small = [t - wide[SUB * n : SUB * (n + 1)] * t[j : j + 1, :] for n, t in enumerate(small)]
    ts = [
        jnp.concatenate([jnp.where(lane // SUB == m, t, 0.0) for m in range(BLK // SUB)], axis=0)
        for t in small
    ]
    half = BLK // 2
    rows = iota((half, BLK), 0)
    cols = iota((half, BLK), 1)
    size = SUB
    while size < BLK:
        part = cols // size == 2 * (rows // size)
        zero = jnp.zeros((size, BLK), f32)
        prods = [
            dot3(split(jnp.where(part, odd_rows(c, size), 0.0)), split(t)) for c, t in zip(couplings, ts)
        ]
        lowers = []
        for prod, t in zip(prods, ts):
            tall = []
            for m in range(half // size):
                tall += [zero, prod[m * size : (m + 1) * size]]
            lower = odd_rows(t, size)
            lowers.append(lower - dot3(split(lower), split(jnp.concatenate(tall, axis=0))))
        new = []
        for lower, t in zip(lowers, ts):
            pieces = []
            for m in range(half // size):
                pieces += [t[2 * m * size : (2 * m + 1) * size], lower[m * size : (m + 1) * size]]
            new.append(jnp.concatenate(pieces, axis=0))
        ts = new
        size *= 2
    return [split(t) for t in ts]


def mixer_body(q_ref, k_ref, v_ref, halo_ref, bl_ref, dl_ref, rate_ref, cq_ref, ck_ref, cv_ref,
               map_ref, local_ref, lift_ref, pad_ref, cum_ref, beta_ref, spread_ref):
    step = pl.program_id(0)
    row = iota((BLK, BLK), 0)
    col = iota((BLK, BLK), 1)

    @pl.when(step == 0)
    def _():
        fill_spread(spread_ref)
        x = dl_ref[...]
        soft = jnp.maximum(x, 0.0) + jnp.log1p(jnp.exp(-jnp.abs(x)))
        square = iota((8, 8), 0) == iota((8, 8), 1)
        rate = jnp.sum(jnp.where(square, rate_ref[...], 0.0), axis=1, keepdims=True)
        decay = jnp.maximum(-rate * soft, -110.0)
        upper = (row <= col).astype(f32)
        for b in range(2):
            cum_ref[b] = lax.dot_general(decay[:, b * BLK : (b + 1) * BLK], upper, (((1,), (0,)), ((), ())),
                                         precision=lax.Precision.HIGHEST, preferred_element_type=f32)
            beta_ref[b] = 1.0 / (1.0 + jnp.exp(-bl_ref[:, b * BLK : (b + 1) * BLK]))

    kw = KH * HD

    def halo(at, width):
        return halo_ref[:, pl.ds(pl.multiple_of(at + step * width, width), width)]

    queries = conv_silu(q_ref, halo(0, kw), cq_ref, pad_ref)
    keys = conv_silu(k_ref, halo(4 * HD, kw), ck_ref, pad_ref)
    values = conv_silu(v_ref, halo(8 * HD, 2 * kw), cv_ref, pad_ref)
    heads = 2 * KH
    rows = {}
    for b in range(2):
        for i in range(heads):
            rows[b, i] = (
                cum_ref[b, pl.ds(heads * step + i, 1), :],
                beta_ref[b, pl.ds(heads * step + i, 1), :],
            )
    keyed = [(b, i) for b in range(2) for i in range(heads)]
    wide = [r for key in keyed for r in rows[key]]
    tall = jnp.concatenate(wide + [jnp.zeros((BLK - len(wide), BLK), f32)], axis=0).T

    res = {}
    qs, ks, grams, scores, masks, couplings = {}, {}, {}, {}, {}, []
    for c in range(KH):
        unit = keys[:, c * HD : (c + 1) * HD]
        unit = unit * lax.rsqrt(jnp.sum(unit * unit, axis=1, keepdims=True) + EPS)
        for b in range(2):
            qs[b, c] = queries[b * BLK : (b + 1) * BLK, c * HD : (c + 1) * HD]
            ks[b, c] = unit[b * BLK : (b + 1) * BLK]
            kb = split(ks[b, c])
            grams[b, c] = dot3(kb, kb, NT)
            scores[b, c] = dot(qs[b, c].astype(bf16), kb[0], NT)
    for n, (b, i) in enumerate(keyed):
        spread = tall[:, 2 * n : 2 * n + 1] - rows[b, i][0]
        masks[b, i] = jnp.where(row >= col, jnp.exp(jnp.where(row >= col, spread, 0.0)), 0.0)
        couplings.append(
            jnp.where(row > col, tall[:, 2 * n + 1 : 2 * n + 2] * grams[b, i // 2] * masks[b, i], 0.0)
        )
    invs = inverses(couplings, spread_ref)
    for n, (b, i) in enumerate(keyed):
        cum_c = tall[:, 2 * n : 2 * n + 1]
        beta_c = tall[:, 2 * n + 1 : 2 * n + 2]
        qb, kb = qs[b, i // 2], ks[b, i // 2]
        vb = values[b * BLK : (b + 1) * BLK, i * HD : (i + 1) * HD]
        grow = jnp.exp(cum_c)
        last = cum_c[BLK - 1 : BLK, :]
        key_tail = (kb * jnp.exp(last - cum_c)).astype(bf16)
        rhs = jnp.concatenate([beta_c * vb, (beta_c * grow) * kb], axis=1)
        solved = dot3(invs[n], split(rhs)).astype(bf16)
        near = dot((scores[b, i // 2] * masks[b, i]).astype(bf16), solved)
        local = near[:, :HD]
        lift = grow * qb - near[:, HD:]
        both = dot(solved, key_tail, TN)
        res[b, i] = (local, lift, jnp.exp(last), both)
    for i in range(heads):
        l0, f0, t0, both0 = res[0, i]
        l1, f1, t1, both1 = res[1, i]
        w0, gone0 = both0[:HD], both0[HD:]
        w1, gone1 = both1[:HD], both1[HD:]
        first = both0.astype(bf16)
        joined = dot(first, gone1.astype(bf16))
        w = t1 * w0 - joined[:HD] + w1
        m = (t0 * t1) * (row == col).astype(f32) - t0 * gone1 - t1 * gone0 + joined[HD:]
        moved = dot(f1.astype(bf16), first, NT)
        local_ref[i, 0:BLK] = l0
        local_ref[i, BLK:TOK] = l1 + moved[:, :HD]
        lift_ref[i, 0:BLK] = f0.astype(bf16)
        lift_ref[i, BLK:TOK] = (t0 * f1 - moved[:, HD:]).astype(bf16)
        map_ref[i, 0:HD] = m.astype(bf16)
        map_ref[i, HD : 2 * HD] = w.astype(bf16)


def mixer_blocks(q, k, v, halo, beta_t, decay_t, rate, cq, ck, cv):
    w = KH * HD
    heads = 2 * KH
    cols = lambda s: (0, s)
    return pl.pallas_call(
        mixer_body,
        grid=(4 // KH,),
        in_specs=[
            pl.BlockSpec((TOK, w), cols),
            pl.BlockSpec((TOK, w), cols),
            pl.BlockSpec((TOK, 2 * w), cols),
        ]
        + in_vmem(4)
        + [
            pl.BlockSpec((4, w), cols),
            pl.BlockSpec((4, w), cols),
            pl.BlockSpec((4, 2 * w), cols),
        ],
        out_specs=[
            pl.BlockSpec((heads, 2 * HD, HD), lambda s: (s, 0, 0)),
            pl.BlockSpec((heads, TOK, HD), lambda s: (s, 0, 0)),
            pl.BlockSpec((heads, TOK, HD), lambda s: (s, 0, 0)),
        ],
        out_shape=[
            jax.ShapeDtypeStruct((NEAR, 2 * HD, HD), bf16),
            jax.ShapeDtypeStruct((8, TOK, HD), f32),
            jax.ShapeDtypeStruct((8, TOK, HD), bf16),
        ],
        scratch_shapes=[
            pltpu.VMEM((TOK + HALO, 2 * w), f32),
            pltpu.VMEM((2, 8, BLK), f32),
            pltpu.VMEM((2, 8, BLK), f32),
            pltpu.VMEM((BLK, (SUB - 1) * BLK), bf16),
        ],
        compiler_params=vmem(56),
        name="mixer_blocks",
    )(q, k, v, halo, beta_t, decay_t, rate, cq, ck, cv)


def edge_body(q_ref, k_ref, v_ref, out_ref):
    out_ref[:, 0 : 4 * HD] = q_ref[...]
    out_ref[:, 4 * HD : 8 * HD] = k_ref[...]
    out_ref[:, 8 * HD : 16 * HD] = v_ref[...]


def edge_rows(q, k, v):
    last = lambda n: (TOK // HALO - 1, 0)
    return pl.pallas_call(
        edge_body,
        grid=(1,),
        in_specs=[pl.BlockSpec((HALO, a.shape[1]), last) for a in (q, k, v)],
        out_specs=pl.BlockSpec((HALO, 2048), lambda n: (0, 0)),
        out_shape=jax.ShapeDtypeStruct((HALO, 2048), bf16),
        name="edge_rows",
    )(q, k, v)


def in_vmem(count):
    return [pl.BlockSpec(memory_space=pltpu.VMEM)] * count


def vmem(mib):
    return pltpu.CompilerParams(vmem_limit_bytes=mib * 1024 * 1024)


def near_body(in_ref, map_ref, mem_ref, all_ref):
    both = in_ref[0].astype(f32)
    for j in range(1, NEAR):
        hi, lo = split(both)
        map_ref[j - 1] = hi[:HD]
        mem_ref[j - 1] = both[HD:]
        here = in_ref[j]
        both = dot(hi, here[:HD]) + dot(lo, here[:HD])
        both = jnp.concatenate([both[:HD], both[HD:] + here[HD:].astype(f32)], axis=0)
    all_ref[...] = both.astype(bf16)


def near_scan(maps):
    return pl.pallas_call(
        near_body,
        in_specs=in_vmem(1),
        out_shape=[
            jax.ShapeDtypeStruct((NEAR - 1, HD, HD), bf16),
            jax.ShapeDtypeStruct((NEAR - 1, HD, HD), f32),
            jax.ShapeDtypeStruct((2 * HD, HD), bf16),
        ],
        compiler_params=vmem(8),
        name="near_scan",
    )(maps)


def far_body(near_ref, next_ref, last_ref, w_ref, map_ref, mem_ref, out_ref):
    state = last_ref[HD:].astype(f32)
    for ref in (next_ref, near_ref):
        hi, lo = split(state)
        state = dot(hi, ref[:HD]) + dot(lo, ref[:HD]) + ref[HD:].astype(f32)
    hi, lo = split(state)
    out_ref[0] = hi
    for j in range(1, NEAR):
        m = map_ref[j - 1]
        out_ref[j] = (dot(hi, m) + dot(lo, m) + mem_ref[j - 1]).astype(bf16)


def far_scan(totals, weight, maps, memories):
    return pl.pallas_call(
        far_body,
        in_specs=in_vmem(3) + [pl.BlockSpec(memory_space=pl.ANY)] + in_vmem(2),
        out_shape=jax.ShapeDtypeStruct((NEAR, HD, HD), bf16),
        compiler_params=vmem(50),
        name="far_scan",
    )(*totals, weight, maps, memories)


def project_body(s_ref, local_ref, lift_ref, gate_ref, gain_ref, w_ref, out_ref, norm_ref):
    for h in range(8):
        core = local_ref[h] + dot(lift_ref[h], s_ref[h], NT)
        gate = gate_ref[:, h * HD : (h + 1) * HD].astype(f32)
        ms = jnp.sum(core * core, axis=1, keepdims=True) * (1.0 / HD)
        act = gate / (1.0 + jnp.exp(-gate))
        norm_ref[:, h * HD : (h + 1) * HD] = (core * lax.rsqrt(ms + EPS) * gain_ref[...] * act).astype(bf16)
    for n in range(4):
        out = dot(norm_ref[...], w_ref[:, n * QW : (n + 1) * QW]).astype(bf16)
        for e in range(EXP):
            out_ref[e, :, n * QW : (n + 1) * QW] = out[e * ROWS : (e + 1) * ROWS]


def project(states, local, lift, gate, gain, weight):
    return pl.pallas_call(
        project_body,
        in_specs=in_vmem(6),
        out_shape=jax.ShapeDtypeStruct((EXP, ROWS, 2048), bf16),
        scratch_shapes=[pltpu.VMEM((TOK, 8 * HD), bf16)],
        compiler_params=vmem(16),
        name="project",
    )(states, local, lift, gate, gain, weight)


def route_body(experts_ref, weights_ref, slot_ref, part_ref, share_ref):
    ids = experts_ref[...]
    weights = weights_ref[...]
    shares = weights / jnp.sum(weights, axis=1, keepdims=True)
    lane = iota((ROWS, DEV), 1)
    token = iota((ROWS, DEV), 0).astype(f32)
    earlier = (iota((ROWS, ROWS), 0) > iota((ROWS, ROWS), 1)).astype(bf16)
    for e in range(2):
        named = jnp.zeros((ROWS, DEV), f32)
        part = jnp.zeros((ROWS, DEV), f32)
        for k in range(PICKS):
            hit = ids[:, k : k + 1] == 2 * lane + e
            named = named + jnp.where(hit, 1.0, 0.0)
            part = part + jnp.where(hit, shares[:, k : k + 1], 0.0)
        rank = dot(earlier, named.astype(bf16))
        for r in range(CAP):
            hit = (named > 0.5) & (rank == float(r))
            used = jnp.sum(jnp.where(hit, 1.0, 0.0), axis=0, keepdims=True)
            tok = jnp.sum(jnp.where(hit, token, 0.0), axis=0, keepdims=True)
            share = jnp.sum(jnp.where(hit, part, 0.0), axis=0, keepdims=True)
            for q in range(NQ):
                j = q * 2 * CAP + e * CAP + r
                slot_ref[j : j + 1, :] = jnp.where(used > 0.5, tok + float(ROWS * q), -1.0)
                share_ref[j : j + 1, :] = share
    slots = slot_ref[...]
    shs = share_ref[...]
    lane2 = iota((CH, NQ * ROWS), 1).astype(f32)
    for g in range(DEV // 8):
        tall = [
            jnp.where(slots[:, d : d + 1] == lane2, shs[:, d : d + 1], 0.0)
            for d in range(8 * g, 8 * g + 8)
        ]
        part_ref[:, g * 8 * CH : (g + 1) * 8 * CH] = jnp.concatenate(tall, axis=0).T.astype(bf16)


def route(experts, weights):
    return pl.pallas_call(
        route_body,
        out_shape=[
            jax.ShapeDtypeStruct((CH, DEV), f32),
            jax.ShapeDtypeStruct((NQ * ROWS, DEV * CH), bf16),
        ],
        scratch_shapes=[pltpu.VMEM((CH, DEV), f32)],
        compiler_params=vmem(16),
        name="route",
    )(experts, weights)


def dispatch_body(parts_ref, res_ref, gain_ref, slot_ref, mix_ref, out_ref, stack_ref):
    total = parts_ref[0].astype(f32)
    for e in range(1, EXP):
        total = total + parts_ref[e].astype(f32)
    mixed = (res_ref[...].astype(f32) + total).astype(bf16)
    mix_ref[...] = mixed
    m = mixed.astype(f32)
    ms = jnp.sum(m * m, axis=1, keepdims=True) * (1.0 / (NQ * QW))
    normed = (m * lax.rsqrt(ms + EPS) * gain_ref[...]).astype(bf16)
    for q in range(NQ):
        stack_ref[q * ROWS : (q + 1) * ROWS, :] = normed[:, q * QW : (q + 1) * QW]
    slots = slot_ref[...]
    lane = iota((CH, NQ * ROWS), 1).astype(f32)
    each = 16
    for n in range(DEV // each):
        pick = jnp.concatenate(
            [
                jnp.where(slots[:, d : d + 1] == lane, 1.0, 0.0).astype(bf16)
                for d in range(n * each, (n + 1) * each)
            ],
            axis=0,
        )
        out_ref[n * each * CH : (n + 1) * each * CH, :] = dot(pick, stack_ref[...]).astype(bf16)


def dispatch(parts, residual, gain, slots):
    return pl.pallas_call(
        dispatch_body,
        in_specs=in_vmem(4),
        out_shape=[
            jax.ShapeDtypeStruct((ROWS, 2048), bf16),
            jax.ShapeDtypeStruct((DEV * CH, QW), bf16),
        ],
        scratch_shapes=[pltpu.VMEM((NQ * ROWS, QW), bf16)],
        compiler_params=vmem(16),
        name="dispatch",
    )(parts, residual, gain, slots)


GS = 4
GR = GS * CH
PR = GS * CAP


def expert_body(in_ref, gate_ref, up_ref, down_ref, out_ref, x_ref, y_ref):
    def place(n):
        rest = n % CH
        return (rest // CAP) * PR + (n // CH) * CAP + rest % CAP

    perm = (iota((GR, GR), 0) == place(iota((GR, GR), 1))).astype(bf16)
    perm_t = (iota((GR, GR), 1) == place(iota((GR, GR), 0))).astype(bf16)
    pairs = DEV // (2 * GS)

    def load(i, _):
        a = dot(perm, in_ref[pl.ds(2 * GR * i, GR), :])
        b = dot(perm, in_ref[pl.ds(2 * GR * i + GR, GR), :])
        for q in range(NQ):
            for e in range(2):
                at = (2 * q + e) * PR
                both = jnp.concatenate([a[at : at + PR], b[at : at + PR]], axis=0).astype(bf16)
                x_ref[e, pl.ds(2 * PR * i, 2 * PR), q * QW : (q + 1) * QW] = both
        return 0

    lax.fori_loop(0, pairs, load, 0, unroll=4)
    for e in range(2):
        x = x_ref[e]
        g = dot(x, gate_ref[e])
        u = dot(x, up_ref[e])
        inner = (g / (1.0 + jnp.exp(-g)) * u).astype(bf16)
        y_ref[e] = dot(inner, down_ref[e]).astype(bf16)

    def store(i, _):
        halves = ([], [])
        for q in range(NQ):
            for e in range(2):
                both = y_ref[e, pl.ds(2 * PR * i, 2 * PR), q * QW : (q + 1) * QW].astype(f32)
                halves[0].append(both[:PR])
                halves[1].append(both[PR:])
        for h in range(2):
            z = jnp.concatenate(halves[h], axis=0).astype(bf16)
            out_ref[pl.ds(2 * GR * i + GR * h, GR), :] = dot(perm_t, z).astype(bf16)
        return 0

    lax.fori_loop(0, pairs, store, 0, unroll=4)


def experts_mlp(arrived, gate, up, down):
    return pl.pallas_call(
        expert_body,
        in_specs=in_vmem(4),
        out_shape=jax.ShapeDtypeStruct((DEV * CH, QW), bf16),
        scratch_shapes=[
            pltpu.VMEM((2, DEV * CAP, 2048), bf16),
            pltpu.VMEM((2, DEV * CAP, 2048), bf16),
        ],
        compiler_params=vmem(26),
        name="experts_mlp",
    )(arrived, gate, up, down)


def combine_body(part_ref, back_ref, out_ref):
    acc = dot(part_ref[...], back_ref[...])
    for q in range(NQ):
        out_ref[:, q * QW : (q + 1) * QW] = acc[q * ROWS : (q + 1) * ROWS, :].astype(bf16)


def combine(part, back):
    return pl.pallas_call(
        combine_body,
        in_specs=in_vmem(2),
        out_shape=jax.ShapeDtypeStruct((ROWS, 2048), bf16),
        compiler_params=vmem(8),
        name="combine",
    )(part, back)


def exchange(rows):
    chunks = rows.reshape(DEV, CH, QW)
    moved = lax.all_to_all(chunks, ("seq", "exp"), split_axis=0, concat_axis=0, tiled=True)
    return moved.reshape(DEV * CH, QW)


def body(
    query_proj,
    key_proj,
    value_proj,
    result_valve_maps,
    beta_logit,
    decay_logit,
    decay_rate,
    conv_query,
    conv_key,
    conv_value,
    norm_gain,
    output_weight,
    residual,
    post_gain,
    route_experts,
    route_weights,
    expert_gate,
    expert_up,
    expert_down,
):
    edge = edge_rows(query_proj, key_proj, value_proj)
    halo = lax.ppermute(edge, "seq", [(s, s + 1) for s in range(SEQ - 1)])
    slots, share = route(route_experts, route_weights)
    maps, local, lift = mixer_blocks(
        query_proj,
        key_proj,
        value_proj,
        halo,
        beta_logit.T,
        decay_logit.T,
        decay_rate[None, :],
        conv_query,
        conv_key,
        conv_value,
    )
    near = [[g * NEAR + j for j in range(NEAR)] for g in range(FAR)]

    def swap(array):
        return lax.all_to_all(array, "seq", split_axis=0, concat_axis=0, axis_index_groups=near, tiled=True)

    before, memories, total = near_scan(swap(maps))
    totals = [
        lax.ppermute(total, "seq", [(s, s + k * NEAR) for s in range(SEQ - k * NEAR)]) for k in range(1, FAR)
    ]
    states = swap(far_scan(totals, output_weight, before, memories))
    parts = project(
        states, local, lift, result_valve_maps, norm_gain[None, :], output_weight
    )
    parts = lax.all_to_all(parts, "exp", split_axis=0, concat_axis=0, tiled=True)
    mixer_out, outgoing = dispatch(parts, residual, post_gain[None, :], slots)
    finished = experts_mlp(exchange(outgoing), expert_gate, expert_up, expert_down)
    return (mixer_out, combine(share, exchange(finished)))


def solution(mesh):
    wide = P("seq", "exp")
    rows = P(("seq", "exp"), None)
    whole = P(("seq", "exp"), None, None)
    taps = P(None, "exp")
    in_specs = (wide, wide, wide, wide, wide, wide, P("exp"), taps, taps, taps, P(), P("exp", None), rows, P(), rows, rows, whole, whole, whole)
    return jax.shard_map(body, mesh=mesh, in_specs=in_specs, out_specs=(rows, rows), check_vma=False)
```

```python
import jax
import jax.numpy as jnp
from jax import lax
from jax.experimental import pallas as pl
from jax.experimental.pallas import tpu as pltpu
from jax.sharding import PartitionSpec as P

f32 = jnp.float32
bf16 = jnp.bfloat16
EPS = 1e-06
HD = 128
BLK = 128
SUB = 16
KH = 2
TOK = 256
HALO = 8
SEQ = 32
NEAR = 8
FAR = SEQ // NEAR
EXP = 4
DEV = SEQ * EXP
ROWS = 64
PICKS = 10
CAP = 6
NQ = 4
CH = 2 * CAP * NQ
QW = 512
FF = 512
VMEM = 56 * 1024 * 1024


def iota(shape, dim):
    return lax.broadcasted_iota(jnp.int32, shape, dim)


def split(a):
    hi = a.astype(bf16)
    return hi, (a - hi.astype(f32)).astype(bf16)


def dot(a, b, dims=((1,), (0,))):
    return lax.dot_general(a, b, (dims, ((), ())), preferred_element_type=f32)


def dot3(a, b, dims=((1,), (0,))):
    return dot(a[0], b[0], dims) + (dot(a[0], b[1], dims) + dot(a[1], b[0], dims))


NT = ((1,), (1,))
TN = ((0,), (0,))


def conv_silu(ref, halo, taps_ref, pad_ref):
    width = ref.shape[1]
    pad_ref[0:HALO, 0:width] = halo.astype(f32)
    pad_ref[HALO : HALO + TOK, 0:width] = ref[...].astype(f32)
    run = taps_ref[0:1, :] * pad_ref[HALO - 3 : HALO - 3 + TOK, 0:width]
    for j in range(1, 4):
        run = run + taps_ref[j : j + 1, :] * pad_ref[HALO - 3 + j : HALO - 3 + j + TOK, 0:width]
    return run / (1.0 + jnp.exp(-run))


def odd_rows(x, size):
    return jnp.concatenate(
        [x[m * size : (m + 1) * size] for m in range(1, BLK // size, 2)], axis=0
    )


def fill_spread(ref):
    ahead = iota((BLK, BLK), 0) - SUB * (iota((BLK, BLK), 1) // SUB)
    for j in range(SUB - 1):
        ref[:, j * BLK : (j + 1) * BLK] = (ahead == j).astype(bf16)


def inverses(couplings, spread_ref):
    count = len(couplings)
    lane = iota((SUB, BLK), 1)
    sub = iota((SUB, BLK), 0)
    packs = []
    for c in couplings:
        pack = jnp.zeros((SUB, BLK), f32)
        for m in range(BLK // SUB):
            pack = jnp.where(lane // SUB == m, c[SUB * m : SUB * (m + 1)], pack)
        packs.append(pack)
    hi, lo = split(jnp.concatenate(packs, axis=0))
    small = [(lane % SUB == sub).astype(f32)] * count
    for j in range(SUB - 1):
        span = slice(j * BLK, (j + 1) * BLK)
        wide = dot(hi, spread_ref[:, span]) + dot(lo, spread_ref[:, span])
        small = [t - wide[SUB * n : SUB * (n + 1)] * t[j : j + 1, :] for n, t in enumerate(small)]
    ts = [
        jnp.concatenate([jnp.where(lane // SUB == m, t, 0.0) for m in range(BLK // SUB)], axis=0)
        for t in small
    ]
    half = BLK // 2
    rows = iota((half, BLK), 0)
    cols = iota((half, BLK), 1)
    size = SUB
    while size < BLK:
        part = cols // size == 2 * (rows // size)
        zero = jnp.zeros((size, BLK), f32)
        prods = [
            dot3(split(jnp.where(part, odd_rows(c, size), 0.0)), split(t)) for c, t in zip(couplings, ts)
        ]
        lowers = []
        for prod, t in zip(prods, ts):
            tall = []
            for m in range(half // size):
                tall += [zero, prod[m * size : (m + 1) * size]]
            lower = odd_rows(t, size)
            lowers.append(lower - dot3(split(lower), split(jnp.concatenate(tall, axis=0))))
        new = []
        for lower, t in zip(lowers, ts):
            pieces = []
            for m in range(half // size):
                pieces += [t[2 * m * size : (2 * m + 1) * size], lower[m * size : (m + 1) * size]]
            new.append(jnp.concatenate(pieces, axis=0))
        ts = new
        size *= 2
    return [split(t) for t in ts]


def mixer_body(q_ref, k_ref, v_ref, halo_ref, bl_ref, dl_ref, rate_ref, cq_ref, ck_ref, cv_ref,
               map_ref, local_ref, lift_ref, pad_ref, cum_ref, beta_ref, spread_ref):
    step = pl.program_id(0)
    row = iota((BLK, BLK), 0)
    col = iota((BLK, BLK), 1)

    @pl.when(step == 0)
    def _():
        fill_spread(spread_ref)
        x = dl_ref[...]
        soft = jnp.maximum(x, 0.0) + jnp.log1p(jnp.exp(-jnp.abs(x)))
        square = iota((8, 8), 0) == iota((8, 8), 1)
        rate = jnp.sum(jnp.where(square, rate_ref[...], 0.0), axis=1, keepdims=True)
        decay = jnp.maximum(-rate * soft, -110.0)
        upper = (row <= col).astype(f32)
        for b in range(2):
            cum_ref[b] = lax.dot_general(decay[:, b * BLK : (b + 1) * BLK], upper, (((1,), (0,)), ((), ())),
                                         precision=lax.Precision.HIGHEST, preferred_element_type=f32)
            beta_ref[b] = 1.0 / (1.0 + jnp.exp(-bl_ref[:, b * BLK : (b + 1) * BLK]))

    kw = KH * HD

    def halo(at, width):
        return halo_ref[:, pl.ds(pl.multiple_of(at + step * width, width), width)]

    queries = conv_silu(q_ref, halo(0, kw), cq_ref, pad_ref)
    keys = conv_silu(k_ref, halo(4 * HD, kw), ck_ref, pad_ref)
    values = conv_silu(v_ref, halo(8 * HD, 2 * kw), cv_ref, pad_ref)
    heads = 2 * KH
    rows = {}
    for b in range(2):
        for i in range(heads):
            rows[b, i] = (
                cum_ref[b, pl.ds(heads * step + i, 1), :],
                beta_ref[b, pl.ds(heads * step + i, 1), :],
            )
    keyed = [(b, i) for b in range(2) for i in range(heads)]
    wide = [r for key in keyed for r in rows[key]]
    tall = jnp.concatenate(wide + [jnp.zeros((BLK - len(wide), BLK), f32)], axis=0).T

    res = {}
    qs, ks, grams, scores, masks, couplings = {}, {}, {}, {}, {}, []
    for c in range(KH):
        unit = keys[:, c * HD : (c + 1) * HD]
        unit = unit * lax.rsqrt(jnp.sum(unit * unit, axis=1, keepdims=True) + EPS)
        for b in range(2):
            qs[b, c] = queries[b * BLK : (b + 1) * BLK, c * HD : (c + 1) * HD]
            ks[b, c] = unit[b * BLK : (b + 1) * BLK]
            kb = split(ks[b, c])
            grams[b, c] = dot3(kb, kb, NT)
            scores[b, c] = dot3(split(qs[b, c]), kb, NT)
    for n, (b, i) in enumerate(keyed):
        spread = tall[:, 2 * n : 2 * n + 1] - rows[b, i][0]
        masks[b, i] = jnp.where(row >= col, jnp.exp(jnp.where(row >= col, spread, 0.0)), 0.0)
        couplings.append(
            jnp.where(row > col, tall[:, 2 * n + 1 : 2 * n + 2] * grams[b, i // 2] * masks[b, i], 0.0)
        )
    invs = inverses(couplings, spread_ref)
    for n, (b, i) in enumerate(keyed):
        cum_c = tall[:, 2 * n : 2 * n + 1]
        beta_c = tall[:, 2 * n + 1 : 2 * n + 2]
        qb, kb = qs[b, i // 2], ks[b, i // 2]
        vb = values[b * BLK : (b + 1) * BLK, i * HD : (i + 1) * HD]
        grow = jnp.exp(cum_c)
        last = cum_c[BLK - 1 : BLK, :]
        key_tail = split(kb * jnp.exp(last - cum_c))
        rhs = jnp.concatenate([beta_c * vb, (beta_c * grow) * kb], axis=1)
        solved = split(dot3(invs[n], split(rhs)))
        near = dot3(split(scores[b, i // 2] * masks[b, i]), solved)
        local = near[:, :HD]
        lift = grow * qb - near[:, HD:]
        both = dot3(solved, key_tail, TN)
        res[b, i] = (local, lift, jnp.exp(last), both)
    for i in range(heads):
        l0, f0, t0, both0 = res[0, i]
        l1, f1, t1, both1 = res[1, i]
        w0, gone0 = both0[:HD], both0[HD:]
        w1, gone1 = both1[:HD], both1[HD:]
        first = both0.astype(bf16)
        joined = dot(first, gone1.astype(bf16))
        w = t1 * w0 - joined[:HD] + w1
        m = (t0 * t1) * (row == col).astype(f32) - t0 * gone1 - t1 * gone0 + joined[HD:]
        moved = dot(f1.astype(bf16), first, NT)
        local_ref[i, 0:BLK] = l0
        local_ref[i, BLK:TOK] = l1 + moved[:, :HD]
        lift_ref[i, 0:BLK] = f0.astype(bf16)
        lift_ref[i, BLK:TOK] = (t0 * f1 - moved[:, HD:]).astype(bf16)
        map_ref[i, 0:HD] = m.astype(bf16)
        map_ref[i, HD : 2 * HD] = w.astype(bf16)


def mixer_blocks(q, k, v, halo, beta_t, decay_t, rate, cq, ck, cv):
    w = KH * HD
    heads = 2 * KH
    cols = lambda s: (0, s)
    return pl.pallas_call(
        mixer_body,
        grid=(4 // KH,),
        in_specs=[
            pl.BlockSpec((TOK, w), cols),
            pl.BlockSpec((TOK, w), cols),
            pl.BlockSpec((TOK, 2 * w), cols),
        ]
        + in_vmem(4)
        + [
            pl.BlockSpec((4, w), cols),
            pl.BlockSpec((4, w), cols),
            pl.BlockSpec((4, 2 * w), cols),
        ],
        out_specs=[
            pl.BlockSpec((heads, 2 * HD, HD), lambda s: (s, 0, 0)),
            pl.BlockSpec((heads, TOK, HD), lambda s: (s, 0, 0)),
            pl.BlockSpec((heads, TOK, HD), lambda s: (s, 0, 0)),
        ],
        out_shape=[
            jax.ShapeDtypeStruct((NEAR, 2 * HD, HD), bf16),
            jax.ShapeDtypeStruct((8, TOK, HD), f32),
            jax.ShapeDtypeStruct((8, TOK, HD), bf16),
        ],
        scratch_shapes=[
            pltpu.VMEM((TOK + HALO, 2 * w), f32),
            pltpu.VMEM((2, 8, BLK), f32),
            pltpu.VMEM((2, 8, BLK), f32),
            pltpu.VMEM((BLK, (SUB - 1) * BLK), bf16),
        ],
        compiler_params=vmem(56),
        name="mixer_blocks",
    )(q, k, v, halo, beta_t, decay_t, rate, cq, ck, cv)


def edge_body(q_ref, k_ref, v_ref, out_ref):
    out_ref[:, 0 : 4 * HD] = q_ref[...]
    out_ref[:, 4 * HD : 8 * HD] = k_ref[...]
    out_ref[:, 8 * HD : 16 * HD] = v_ref[...]


def edge_rows(q, k, v):
    last = lambda n: (TOK // HALO - 1, 0)
    return pl.pallas_call(
        edge_body,
        grid=(1,),
        in_specs=[pl.BlockSpec((HALO, a.shape[1]), last) for a in (q, k, v)],
        out_specs=pl.BlockSpec((HALO, 2048), lambda n: (0, 0)),
        out_shape=jax.ShapeDtypeStruct((HALO, 2048), bf16),
        name="edge_rows",
    )(q, k, v)


def in_vmem(count):
    return [pl.BlockSpec(memory_space=pltpu.VMEM)] * count


def vmem(mib):
    return pltpu.CompilerParams(vmem_limit_bytes=mib * 1024 * 1024)


def near_body(in_ref, map_ref, mem_ref, all_ref):
    both = in_ref[0].astype(f32)
    for j in range(1, NEAR):
        hi, lo = split(both)
        map_ref[j - 1] = hi[:HD]
        mem_ref[j - 1] = both[HD:]
        here = in_ref[j]
        both = dot(hi, here[:HD]) + dot(lo, here[:HD])
        both = jnp.concatenate([both[:HD], both[HD:] + here[HD:].astype(f32)], axis=0)
    all_ref[...] = both.astype(bf16)


def near_scan(maps):
    return pl.pallas_call(
        near_body,
        in_specs=in_vmem(1),
        out_shape=[
            jax.ShapeDtypeStruct((NEAR - 1, HD, HD), bf16),
            jax.ShapeDtypeStruct((NEAR - 1, HD, HD), f32),
            jax.ShapeDtypeStruct((2 * HD, HD), bf16),
        ],
        compiler_params=vmem(8),
        name="near_scan",
    )(maps)


def far_body(near_ref, next_ref, last_ref, w_ref, map_ref, mem_ref, out_ref):
    state = last_ref[HD:].astype(f32)
    for ref in (next_ref, near_ref):
        hi, lo = split(state)
        state = dot(hi, ref[:HD]) + dot(lo, ref[:HD]) + ref[HD:].astype(f32)
    hi, lo = split(state)
    out_ref[0] = hi
    for j in range(1, NEAR):
        m = map_ref[j - 1]
        out_ref[j] = (dot(hi, m) + dot(lo, m) + mem_ref[j - 1]).astype(bf16)


def far_scan(totals, weight, maps, memories):
    return pl.pallas_call(
        far_body,
        in_specs=in_vmem(3) + [pl.BlockSpec(memory_space=pl.ANY)] + in_vmem(2),
        out_shape=jax.ShapeDtypeStruct((NEAR, HD, HD), bf16),
        compiler_params=vmem(50),
        name="far_scan",
    )(*totals, weight, maps, memories)


def project_body(s_ref, local_ref, lift_ref, gate_ref, gain_ref, w_ref, out_ref, norm_ref):
    for h in range(8):
        core = local_ref[h] + dot(lift_ref[h], s_ref[h], NT)
        gate = gate_ref[:, h * HD : (h + 1) * HD].astype(f32)
        ms = jnp.sum(core * core, axis=1, keepdims=True) * (1.0 / HD)
        act = gate / (1.0 + jnp.exp(-gate))
        norm_ref[:, h * HD : (h + 1) * HD] = (core * lax.rsqrt(ms + EPS) * gain_ref[...] * act).astype(bf16)
    for n in range(4):
        out = dot(norm_ref[...], w_ref[:, n * QW : (n + 1) * QW]).astype(bf16)
        for e in range(EXP):
            out_ref[e, :, n * QW : (n + 1) * QW] = out[e * ROWS : (e + 1) * ROWS]


def project(states, local, lift, gate, gain, weight):
    return pl.pallas_call(
        project_body,
        in_specs=in_vmem(6),
        out_shape=jax.ShapeDtypeStruct((EXP, ROWS, 2048), bf16),
        scratch_shapes=[pltpu.VMEM((TOK, 8 * HD), bf16)],
        compiler_params=vmem(16),
        name="project",
    )(states, local, lift, gate, gain, weight)


def route_body(experts_ref, weights_ref, slot_ref, part_ref, share_ref):
    ids = experts_ref[...]
    weights = weights_ref[...]
    shares = weights / jnp.sum(weights, axis=1, keepdims=True)
    lane = iota((ROWS, DEV), 1)
    token = iota((ROWS, DEV), 0).astype(f32)
    earlier = (iota((ROWS, ROWS), 0) > iota((ROWS, ROWS), 1)).astype(bf16)
    for e in range(2):
        named = jnp.zeros((ROWS, DEV), f32)
        part = jnp.zeros((ROWS, DEV), f32)
        for k in range(PICKS):
            hit = ids[:, k : k + 1] == 2 * lane + e
            named = named + jnp.where(hit, 1.0, 0.0)
            part = part + jnp.where(hit, shares[:, k : k + 1], 0.0)
        rank = dot(earlier, named.astype(bf16))
        for r in range(CAP):
            hit = (named > 0.5) & (rank == float(r))
            used = jnp.sum(jnp.where(hit, 1.0, 0.0), axis=0, keepdims=True)
            tok = jnp.sum(jnp.where(hit, token, 0.0), axis=0, keepdims=True)
            share = jnp.sum(jnp.where(hit, part, 0.0), axis=0, keepdims=True)
            for q in range(NQ):
                j = q * 2 * CAP + e * CAP + r
                slot_ref[j : j + 1, :] = jnp.where(used > 0.5, tok + float(ROWS * q), -1.0)
                share_ref[j : j + 1, :] = share
    slots = slot_ref[...]
    shs = share_ref[...]
    lane2 = iota((CH, NQ * ROWS), 1).astype(f32)
    for g in range(DEV // 8):
        tall = [
            jnp.where(slots[:, d : d + 1] == lane2, shs[:, d : d + 1], 0.0)
            for d in range(8 * g, 8 * g + 8)
        ]
        part_ref[:, g * 8 * CH : (g + 1) * 8 * CH] = jnp.concatenate(tall, axis=0).T.astype(bf16)


def route(experts, weights):
    return pl.pallas_call(
        route_body,
        out_shape=[
            jax.ShapeDtypeStruct((CH, DEV), f32),
            jax.ShapeDtypeStruct((NQ * ROWS, DEV * CH), bf16),
        ],
        scratch_shapes=[pltpu.VMEM((CH, DEV), f32)],
        compiler_params=vmem(16),
        name="route",
    )(experts, weights)


def dispatch_body(parts_ref, res_ref, gain_ref, slot_ref, mix_ref, out_ref, stack_ref):
    total = parts_ref[0].astype(f32)
    for e in range(1, EXP):
        total = total + parts_ref[e].astype(f32)
    mixed = (res_ref[...].astype(f32) + total).astype(bf16)
    mix_ref[...] = mixed
    m = mixed.astype(f32)
    ms = jnp.sum(m * m, axis=1, keepdims=True) * (1.0 / (NQ * QW))
    normed = (m * lax.rsqrt(ms + EPS) * gain_ref[...]).astype(bf16)
    for q in range(NQ):
        stack_ref[q * ROWS : (q + 1) * ROWS, :] = normed[:, q * QW : (q + 1) * QW]
    slots = slot_ref[...]
    lane = iota((CH, NQ * ROWS), 1).astype(f32)
    each = 16
    for n in range(DEV // each):
        pick = jnp.concatenate(
            [
                jnp.where(slots[:, d : d + 1] == lane, 1.0, 0.0).astype(bf16)
                for d in range(n * each, (n + 1) * each)
            ],
            axis=0,
        )
        out_ref[n * each * CH : (n + 1) * each * CH, :] = dot(pick, stack_ref[...]).astype(bf16)


def dispatch(parts, residual, gain, slots):
    return pl.pallas_call(
        dispatch_body,
        in_specs=in_vmem(4),
        out_shape=[
            jax.ShapeDtypeStruct((ROWS, 2048), bf16),
            jax.ShapeDtypeStruct((DEV * CH, QW), bf16),
        ],
        scratch_shapes=[pltpu.VMEM((NQ * ROWS, QW), bf16)],
        compiler_params=vmem(16),
        name="dispatch",
    )(parts, residual, gain, slots)


GS = 4
GR = GS * CH
PR = GS * CAP


def expert_body(in_ref, gate_ref, up_ref, down_ref, out_ref, x_ref, y_ref):
    def place(n):
        rest = n % CH
        return (rest // CAP) * PR + (n // CH) * CAP + rest % CAP

    perm = (iota((GR, GR), 0) == place(iota((GR, GR), 1))).astype(bf16)
    perm_t = (iota((GR, GR), 1) == place(iota((GR, GR), 0))).astype(bf16)
    pairs = DEV // (2 * GS)

    def load(i, _):
        a = dot(perm, in_ref[pl.ds(2 * GR * i, GR), :])
        b = dot(perm, in_ref[pl.ds(2 * GR * i + GR, GR), :])
        for q in range(NQ):
            for e in range(2):
                at = (2 * q + e) * PR
                both = jnp.concatenate([a[at : at + PR], b[at : at + PR]], axis=0).astype(bf16)
                x_ref[e, pl.ds(2 * PR * i, 2 * PR), q * QW : (q + 1) * QW] = both
        return 0

    lax.fori_loop(0, pairs, load, 0, unroll=16)
    for e in range(2):
        x = x_ref[e]
        g = dot(x, gate_ref[e])
        u = dot(x, up_ref[e])
        inner = (g / (1.0 + jnp.exp(-g)) * u).astype(bf16)
        y_ref[e] = dot(inner, down_ref[e]).astype(bf16)

    def store(i, _):
        halves = ([], [])
        for q in range(NQ):
            for e in range(2):
                both = y_ref[e, pl.ds(2 * PR * i, 2 * PR), q * QW : (q + 1) * QW].astype(f32)
                halves[0].append(both[:PR])
                halves[1].append(both[PR:])
        for h in range(2):
            z = jnp.concatenate(halves[h], axis=0).astype(bf16)
            out_ref[pl.ds(2 * GR * i + GR * h, GR), :] = dot(perm_t, z).astype(bf16)
        return 0

    lax.fori_loop(0, pairs, store, 0, unroll=16)


def experts_mlp(arrived, gate, up, down):
    return pl.pallas_call(
        expert_body,
        in_specs=in_vmem(4),
        out_shape=jax.ShapeDtypeStruct((DEV * CH, QW), bf16),
        scratch_shapes=[
            pltpu.VMEM((2, DEV * CAP, 2048), bf16),
            pltpu.VMEM((2, DEV * CAP, 2048), bf16),
        ],
        compiler_params=vmem(26),
        name="experts_mlp",
    )(arrived, gate, up, down)


def combine_body(part_ref, back_ref, out_ref):
    acc = dot(part_ref[...], back_ref[...])
    for q in range(NQ):
        out_ref[:, q * QW : (q + 1) * QW] = acc[q * ROWS : (q + 1) * ROWS, :].astype(bf16)


def combine(part, back):
    return pl.pallas_call(
        combine_body,
        in_specs=in_vmem(2),
        out_shape=jax.ShapeDtypeStruct((ROWS, 2048), bf16),
        compiler_params=vmem(8),
        name="combine",
    )(part, back)


def exchange(rows):
    chunks = rows.reshape(DEV, CH, QW)
    moved = lax.all_to_all(chunks, ("seq", "exp"), split_axis=0, concat_axis=0, tiled=True)
    return moved.reshape(DEV * CH, QW)


def body(
    query_proj,
    key_proj,
    value_proj,
    result_valve_maps,
    beta_logit,
    decay_logit,
    decay_rate,
    conv_query,
    conv_key,
    conv_value,
    norm_gain,
    output_weight,
    residual,
    post_gain,
    route_experts,
    route_weights,
    expert_gate,
    expert_up,
    expert_down,
):
    edge = edge_rows(query_proj, key_proj, value_proj)
    halo = lax.ppermute(edge, "seq", [(s, s + 1) for s in range(SEQ - 1)])
    slots, share = route(route_experts, route_weights)
    maps, local, lift = mixer_blocks(
        query_proj,
        key_proj,
        value_proj,
        halo,
        beta_logit.T,
        decay_logit.T,
        decay_rate[None, :],
        conv_query,
        conv_key,
        conv_value,
    )
    near = [[g * NEAR + j for j in range(NEAR)] for g in range(FAR)]

    def swap(array):
        return lax.all_to_all(array, "seq", split_axis=0, concat_axis=0, axis_index_groups=near, tiled=True)

    before, memories, total = near_scan(swap(maps))
    totals = [
        lax.ppermute(total, "seq", [(s, s + k * NEAR) for s in range(SEQ - k * NEAR)]) for k in range(1, FAR)
    ]
    states = swap(far_scan(totals, output_weight, before, memories))
    parts = project(
        states, local, lift, result_valve_maps, norm_gain[None, :], output_weight
    )
    parts = lax.all_to_all(parts, "exp", split_axis=0, concat_axis=0, tiled=True)
    mixer_out, outgoing = dispatch(parts, residual, post_gain[None, :], slots)
    finished = experts_mlp(exchange(outgoing), expert_gate, expert_up, expert_down)
    return (mixer_out, combine(share, exchange(finished)))


def solution(mesh):
    wide = P("seq", "exp")
    rows = P(("seq", "exp"), None)
    whole = P(("seq", "exp"), None, None)
    taps = P(None, "exp")
    in_specs = (wide, wide, wide, wide, wide, wide, P("exp"), taps, taps, taps, P(), P("exp", None), rows, P(), rows, rows, whole, whole, whole)
    return jax.shard_map(body, mesh=mesh, in_specs=in_specs, out_specs=(rows, rows), check_vma=False)
```
